512 devices in a mesh: shard: 128 (over z, y, core), rep: 4 (over x).
Axes of the slice: x: 4, y: 8, z: 8, core: 2. Of those that a mesh axis runs over, the one named last changes fastest.
Arguments:
- embeddings: bfloat16 [262144, 1024], P('shard'), may hold values from -200 to 200
- labels: int32 [262144], P('shard'), may hold values from 0 to 255, never falling along the last dimension, each value on 1 to 8193 neighbouring positions
Outputs:
- best_similarity: float32 [262144], P('shard')
The draws below stay inside these ranges and needn't reach their ends.
Inputs may be any that keep to these rules, and one draw needn't show every extreme that they name: labels never fall along the rows; each cluster holds at most 8193 consecutive rows, and one cluster holds exactly that many.
All inputs are finite; a program needn't handle non-finite values.
Results may differ from the reference program's by a relative error of at most 0.00063.
Values may be sent and summed in bfloat16 or wider, within the bound.
A program may use at most 64 MiB of HBM per device.

```python
import math
import jax
import jax.numpy as jnp
import numpy as np
from jax import lax

D = 1024
TOK_DEV = 2048
LOOK = 4
ROWS = 262144
CLUSTERS = 256


def draw_embeddings(key, part):
    key_noise = jax.random.fold_in(key, 11)
    key_offset = jax.random.fold_in(key, 12)
    key_weight = jax.random.fold_in(key, 13)
    noise = jax.random.normal(key_noise, (ROWS, D), jnp.float32)
    offset = jax.random.randint(key_offset, (ROWS,), 1, LOOK * TOK_DEV + 1)
    source = (jnp.arange(ROWS, dtype=jnp.int32) - offset) % ROWS
    weight = jax.random.uniform(key_weight, (ROWS, 1), jnp.float32, 0.2, 1.5)
    mixed = noise + weight * noise[source]
    return mixed.astype(jnp.bfloat16)


def split_up(count, total, most, skew):
    weights = [(1 << 20) // math.isqrt(grade ** skew) + 1 for grade in range(2, count + 1)]
    spare, given = total - most - (count - 1), [1] * (count - 1)
    while spare > 0:
        free = [i for i in range(count - 1) if given[i] < most]
        mass, left = sum([weights[i] for i in free]), spare
        for i in free:
            more = min(most - given[i], max(1, left * weights[i] // mass), spare)
            given[i] = given[i] + more
            spare = spare - more
    return np.array([most] + given)


def ragged_sizes(key, number_of, total, bound, skew):
    if number_of == 2:
        one = jax.random.randint(key, (), max(1, total - bound), min(bound, total - 1) + 1)
        return jnp.stack([one, total - one])
    sizes = jnp.asarray(split_up(number_of, total, bound, skew), jnp.int32)
    couples = (number_of - 1) // 2
    source_of, receiver = sizes[1:1 + 2 * couples:2], sizes[2:2 + 2 * couples:2]
    slack = jnp.minimum(source_of - 1, bound - receiver)
    shifted = jax.random.randint(jax.random.fold_in(key, 1), (couples,), 0, 1 << 20) % (slack + 1)
    sizes = sizes.at[1:1 + 2 * couples:2].set(source_of - shifted).at[2:2 + 2 * couples:2].set(receiver + shifted)
    return sizes[jax.random.permutation(jax.random.fold_in(key, 2), number_of)]


def setup_inputs(seed: int = 0) -> dict:
    seeds = jax.random.split(jax.random.key(seed), 3)
    return {
        "embeddings": draw_embeddings(jax.random.fold_in(seeds[2], 71), 0),
        "labels": jnp.searchsorted(jnp.cumsum(ragged_sizes(seeds[1], CLUSTERS, ROWS, LOOK * TOK_DEV + 1, 2)), jnp.arange(ROWS), side="right").astype(jnp.int32),
    }


def normalize(values):
    as_float = values.astype(jnp.float32)
    inverse = lax.rsqrt(lax.optimization_barrier(jnp.mean(as_float * as_float, axis=1, keepdims=True)) + 1e-06)
    return (as_float * inverse / math.sqrt(values.shape[1])).astype(jnp.bfloat16)

def reference(embeddings, labels):
    unit_rows = normalize(embeddings)
    reach = LOOK * TOK_DEV
    padded_rows = jnp.concatenate([jnp.zeros((reach, D), jnp.bfloat16), unit_rows], axis=0)
    padded_labels = jnp.concatenate([jnp.full((reach,), -1, jnp.int32), labels.astype(jnp.int32)], axis=0)

    def one_block(block):
        start_row = (block * TOK_DEV).astype(jnp.int32)
        queries = lax.dynamic_slice_in_dim(unit_rows, start_row, TOK_DEV, 0)
        query_labels = lax.dynamic_slice_in_dim(labels.astype(jnp.int32), start_row, TOK_DEV, 0)
        query_pos = start_row + jnp.arange(TOK_DEV, dtype=jnp.int32)
        keys = lax.dynamic_slice_in_dim(padded_rows, start_row, reach + TOK_DEV, 0)
        key_labels = lax.dynamic_slice_in_dim(padded_labels, start_row, reach + TOK_DEV, 0)
        key_pos = start_row - reach + jnp.arange(reach + TOK_DEV, dtype=jnp.int32)
        scores = lax.dot_general(queries, keys, (((1,), (1,)), ((), ())), preferred_element_type=jnp.float32)
        keep = (key_labels[None, :] == query_labels[:, None]) & (key_pos[None, :] < query_pos[:, None])
        return lax.optimization_barrier(jnp.max(jnp.where(keep, scores, jnp.float32(-1.0)), axis=1))
    blocks = lax.map(one_block, jnp.arange(ROWS // TOK_DEV, dtype=jnp.int32))
    return blocks.reshape(ROWS)
```

```python
import functools

import jax
import jax.numpy as jnp
from jax import lax
from jax.experimental import pallas as pl
from jax.experimental.pallas import tpu as pltpu
from jax.sharding import PartitionSpec as P

MESH = pl.DeviceIdType.MESH
NT = (((1,), (1,)), ((), ()))
BLOCK = 128
SUB = 32
STEPS = 4
PER = BLOCK // SUB
PIECES = STEPS * PER
WINDOW = 4
LAG = 2

OWN = 0
KEYS = 2048
KEY_STEP = 3 * BLOCK
QRY = KEYS + STEPS * KEY_STEP
SIDE = QRY + STEPS * 2 * BLOCK
TOTAL = SIDE + STEPS * 2 * BLOCK

Y_KEY, Y_QRY, X_KEY, X_QRY, S_KEY, S_QRY_A, S_QRY_X, MISC = range(8)


def kernel(shards, emb, labels, out, buf, klab, qlab, acc, lab, res, got_t, got_c, got_r, load_sem, send, recv):
    shard = lax.axis_index("shard")
    rep = lax.axis_index("rep")
    core = lax.rem(shard, 2)
    other = 1 - core
    chip2 = shard - core
    ahead = lax.rem(chip2 + 2, shards)
    behind = lax.rem(chip2 + shards - 2, shards)
    x_key = rep + 1 - 2 * lax.rem(rep, 2)
    x_qry = 3 - rep
    fwd, fwd_c = (ahead + core, rep), (ahead + other, rep)
    bwd, bwd_c = (behind + core, rep), (behind + other, rep)
    sib = (chip2 + other, rep)
    across = [(shard, lax.rem(rep + d, 4)) for d in (1, 2, 3)]

    def copy(src, dst, kind, index, device):
        return pltpu.make_async_remote_copy(
            src_ref=src,
            dst_ref=dst,
            send_sem=send.at[kind, index],
            recv_sem=recv.at[kind, index],
            device_id=device,
            device_id_type=MESH,
        )

    def rows(start, count):
        return pl.ds(pl.multiple_of(start, SUB), count)

    def at(start, count=SUB):
        return buf.at[rows(start, count)]

    def key_step(q):
        return STEPS - 1 - q // PER

    def key_slot(q, slot):
        return KEYS + key_step(q) * KEY_STEP + slot * BLOCK + (q % PER) * SUB

    def qry_slot(base, q, slot):
        return base + (q // PER) * 2 * BLOCK + slot * BLOCK + (q % PER) * SUB

    def y_key(q):
        src = (4 * key_step(q) + rep) * BLOCK + (q % PER) * SUB
        return copy(at(src), at(key_slot(q, 1)), Y_KEY, q, fwd)

    def y_qry(q):
        src = (4 * (q // PER) + rep) * BLOCK + (q % PER) * SUB
        return copy(at(src), at(qry_slot(QRY, q, 0)), Y_QRY, q, bwd)

    def s_key(q):
        return copy(at(key_slot(q, 1)), at(key_slot(q, 0)), S_KEY, q, sib)

    def xk(q):
        return copy(at(key_slot(q, 1)), at(key_slot(q, 2)), X_KEY, q, (shard, x_key))

    def xq(q):
        return copy(at(qry_slot(QRY, q, 0)), at(qry_slot(QRY, q, 1)), X_QRY, q, (shard, x_qry))

    def s_qry(q, slot):
        kind = (S_QRY_A, S_QRY_X)[slot]
        return copy(at(qry_slot(QRY, q, slot)), at(qry_slot(SIDE, q, slot)), kind, q, sib)

    def label_copies():
        return [copy(labels, lab.at[i], MISC, i, d) for i, d in enumerate((fwd, fwd_c, bwd, bwd_c, sib))]

    def side_block(j):
        return copy(at((4 * j + rep) * BLOCK, BLOCK), at(SIDE + j * BLOCK, BLOCK), MISC, 5 + j, sib)

    def load(b, i):
        r = rows(b * BLOCK, BLOCK)
        return pltpu.make_async_copy(emb.at[r], buf.at[r], load_sem.at[i])

    mine = [4 * j + rep for j in (3, 0, 2, 1)]
    rest = [4 * j + lax.rem(rep + o, 4) for j in range(4) for o in (1, 2, 3)]
    order = mine + rest
    for i, b in enumerate(order):
        load(b, i).start()

    barrier = pltpu.get_barrier_semaphore()
    for device in [fwd, fwd_c, bwd, bwd_c, sib] + across:
        pl.semaphore_signal(barrier, inc=1, device_id=device, device_id_type=MESH)

    def normalize(b):
        @pl.loop(0, BLOCK // 32)
        def _(i):
            r = rows(b * BLOCK + i * 32, 32)
            values = buf[r, :].astype(jnp.float32)
            inverse = lax.rsqrt(jnp.mean(values * values, axis=1, keepdims=True) + 1e-06)
            buf[r, :] = (values * inverse * (1.0 / 32.0)).astype(jnp.bfloat16)

    for i in range(2):
        load(order[i], i).wait()
        normalize(order[i])
    pl.semaphore_wait(barrier, 8)
    for q in range(WINDOW):
        y_key(q).start()
        y_qry(q).start()
    for c in label_copies():
        c.start()
    for i in range(2, 4):
        load(order[i], i).wait()
        normalize(order[i])

    @pl.when(core == 1)
    def _():
        for j in range(4):
            side_block(j).start()

    for i in range(4, 16):
        load(order[i], i).wait()
        normalize(order[i])

    acc[...] = jnp.full_like(acc, -1.0)
    res[...] = jnp.full_like(res, -1.0)
    for c in label_copies():
        c.wait_recv()

    def column(row, start):
        wide = jnp.broadcast_to(row, (BLOCK, BLOCK))
        klab[pl.ds(start, BLOCK), :] = wide.T

    def lab_row(i, r):
        return lab[i, pl.ds(r, 1), :]

    qlab[0:16, :] = labels[...]
    for b in range(16):
        column(labels[b:b + 1, :], b * BLOCK)
    for j in range(4):
        a = 4 * j + rep
        column(lab_row(1, a), KEYS + j * KEY_STEP)
        column(lab_row(0, a), KEYS + j * KEY_STEP + BLOCK)
        column(lab_row(0, 4 * j + x_key), KEYS + j * KEY_STEP + 2 * BLOCK)
        qlab[QRY // BLOCK + 2 * j:QRY // BLOCK + 2 * j + 1, :] = lab_row(2, a)
        qlab[QRY // BLOCK + 2 * j + 1:QRY // BLOCK + 2 * j + 2, :] = lab_row(2, 4 * j + x_qry)

    @pl.when(core == 1)
    def _():
        for j in range(4):
            s = SIDE // BLOCK + 2 * j
            qlab[s:s + 1, :] = lab_row(3, 4 * j + rep)
            qlab[s + 1:s + 2, :] = lab_row(3, 4 * j + x_qry)

    @pl.when(core == 0)
    def _():
        for j in range(4):
            qlab[SIDE // BLOCK + j:SIDE // BLOCK + j + 1, :] = lab_row(4, 4 * j + rep)

    def tile(key, qry, causal=False):
        key = pl.multiple_of(key, BLOCK)
        scores = lax.dot_general(
            buf[pl.ds(key, 256), :], buf[rows(qry, 256), :], NT, preferred_element_type=jnp.float32
        )
        lanes = klab[pl.ds(key, 256), :]
        for g in range(2):
            b = qry // BLOCK + g
            keep = lanes == qlab[pl.ds(b, 1), :]
            if causal:
                key_pos = key + lax.broadcasted_iota(jnp.int32, (256, BLOCK), 0)
                qry_pos = qry + g * BLOCK + lax.broadcasted_iota(jnp.int32, (256, BLOCK), 1)
                keep = keep & (key_pos < qry_pos)
            best = jnp.where(keep, scores[:, g * BLOCK:(g + 1) * BLOCK], jnp.float32(-1.0))
            best = jnp.max(best.reshape(32, 8, BLOCK), axis=0)
            a = pl.ds(pl.multiple_of(b * 8, 8), 8)
            acc[a, :] = jnp.maximum(acc[a, :], best)

    def key_tile(j):
        return KEYS + j * KEY_STEP

    def own_triangle(first):
        @pl.loop(first, 8)
        def _(t):
            tile(first * 256, t * 256, causal=True)

    def cross(lo, hi):
        @pl.when(core == 0)
        def _():
            @pl.loop(lo, hi)
            def _(k):
                for t in range(2):
                    tile(k * 256, SIDE + t * 256)

    def near(j, lo, hi):
        for t in range(lo, hi):
            tile(key_tile(j), OWN + t * 256)

    def far(s):
        j = STEPS - 1 - s
        key = key_tile(j) + BLOCK
        for t in range(0, min(s, j) + 1):
            tile(key, QRY + t * 256)
        for k in range(max(s, j + 1), STEPS):
            tile(key_tile(k) + BLOCK, QRY + s * 256)

        @pl.when(core == 1)
        def _():
            for t in range(0, s + 1):
                tile(key, SIDE + t * 256)
            for k in range(j + 1, STEPS):
                tile(key_tile(k) + BLOCK, SIDE + s * 256)

    def relay(q):
        xq(q).wait_recv()

        @pl.when(core == 0)
        def _():
            s_qry(q, 1).start()

    def service(q):
        y_key(q).wait_recv()
        xk(q).start()
        s_key(q).start()
        y_qry(q).wait_recv()
        xq(q).start()

        @pl.when(core == 0)
        def _():
            s_qry(q, 0).start()

        if q + WINDOW < PIECES:
            y_key(q + WINDOW).start()
            y_qry(q + WINDOW).start()
        if q >= LAG:
            relay(q - LAG)

    def near_ready(s):
        for q in range(PER * s, PER * s + PER):
            s_key(q).wait_recv()

    def far_ready(s):
        for q in range(PER * s, PER * s + PER):
            xk(q).wait_recv()

        @pl.when(core == 1)
        def _():
            for q in range(PER * s, PER * s + PER):
                s_qry(q, 0).wait_recv()
                s_qry(q, 1).wait_recv()

    for q in range(PIECES):
        service(q)
        s, u = q // PER - 1, q % PER
        if q == 0:
            own_triangle(rep)
        elif q == 1:
            own_triangle(7 - rep)

            @pl.when(core == 0)
            def _():
                for j in range(4):
                    side_block(j).wait_recv()
        elif q == 2:
            cross(0, 4)
        elif q == 3:
            cross(4, 8)
            r = SIDE // BLOCK

            @pl.when(core == 0)
            def _():
                for j in range(4):
                    b = (r + j) * 8
                    res[24 + j:25 + j, :] = jnp.max(acc[b:b + 8, :], axis=0, keepdims=True)
                copy(res.at[24:32], got_c, MISC, 9, sib).start()
        else:
            if u == 0:
                near_ready(s)
            near(STEPS - 1 - s, 2 * u, 2 * u + 2)
            if u == 3:
                far_ready(s)
                far(s)

    s = STEPS - 1
    near_ready(s)
    for q in range(PIECES - LAG, PIECES):
        relay(q)
    near(STEPS - 1 - s, 0, 8)
    far_ready(s)
    far(s)

    def reduce_into(dst, block, count):
        for i in range(count):
            b = (block + i) * 8
            res[dst + i:dst + i + 1, :] = jnp.max(acc[b:b + 8, :], axis=0, keepdims=True)

    reduce_into(16, QRY // BLOCK, 8)
    t_same = copy(res.at[16:24], got_t.at[0], MISC, 10, fwd)
    t_same.start()
    t_cross = copy(res.at[24:32], got_t.at[1], MISC, 11, fwd_c)
    c_cross = copy(res.at[24:32], got_c, MISC, 9, sib)

    @pl.when(core == 1)
    def _():
        reduce_into(24, SIDE // BLOCK, 8)
        t_cross.start()

    reduce_into(0, 0, 16)

    def merge(value, b):
        r = pl.ds(b, 1)
        res[r, :] = jnp.maximum(res[r, :], value)

    @pl.when(core == 1)
    def _():
        c_cross.wait_recv()
        for j in range(4):
            merge(got_c[j:j + 1, :], 4 * j + rep)

    def merge_t(i):
        for j in range(4):
            merge(got_t[i, 2 * j:2 * j + 1, :], 4 * j + rep)
            merge(got_t[i, 2 * j + 1:2 * j + 2, :], 4 * j + x_qry)

    t_same.wait_recv()
    merge_t(0)

    @pl.when(core == 0)
    def _():
        t_cross.wait_recv()
        merge_t(1)

    spread = [copy(res.at[0:16], got_r.at[i], MISC, 12 + i, across[i]) for i in range(3)]
    for c in spread:
        c.start()
    for c in spread:
        c.wait_recv()
    out[...] = jnp.maximum(jnp.maximum(res[0:16, :], got_r[0]), jnp.maximum(got_r[1], got_r[2]))

    for q in range(PIECES):
        for c in (y_key(q), y_qry(q), xk(q), xq(q), s_key(q)):
            c.wait_send()
    for c in label_copies() + spread + [t_same]:
        c.wait_send()

    @pl.when(core == 0)
    def _():
        for q in range(PIECES):
            s_qry(q, 0).wait_send()
            s_qry(q, 1).wait_send()
        c_cross.wait_send()

    @pl.when(core == 1)
    def _():
        for j in range(4):
            side_block(j).wait_send()
        t_cross.wait_send()


def solution(mesh):
    shards = mesh.shape["shard"]

    def local(embeddings, labels):
        best = pl.pallas_call(
            functools.partial(kernel, shards),
            out_shape=jax.ShapeDtypeStruct((16, 128), jnp.float32),
            in_specs=[pl.BlockSpec(memory_space=pl.ANY), pl.BlockSpec(memory_space=pltpu.VMEM)],
            out_specs=pl.BlockSpec(memory_space=pltpu.VMEM),
            scratch_shapes=[
                pltpu.VMEM((TOTAL, 1024), jnp.bfloat16),
                pltpu.VMEM((QRY, BLOCK), jnp.int32),
                pltpu.VMEM((TOTAL // BLOCK, BLOCK), jnp.int32),
                pltpu.VMEM((TOTAL // BLOCK * 8, BLOCK), jnp.float32),
                pltpu.VMEM((5, 16, BLOCK), jnp.int32),
                pltpu.VMEM((32, BLOCK), jnp.float32),
                pltpu.VMEM((2, 8, BLOCK), jnp.float32),
                pltpu.VMEM((8, BLOCK), jnp.float32),
                pltpu.VMEM((3, 16, BLOCK), jnp.float32),
                pltpu.SemaphoreType.DMA((16,)),
                pltpu.SemaphoreType.DMA((8, 16)),
                pltpu.SemaphoreType.DMA((8, 16)),
            ],
            compiler_params=pltpu.CompilerParams(
                collective_id=0, has_side_effects=True, vmem_limit_bytes=56 * 2**20
            ),
        )(embeddings, labels.reshape(16, 128))
        return best.reshape(2048)

    placed = (P("shard", None), P("shard"))
    return jax.shard_map(local, mesh=mesh, in_specs=placed, out_specs=P("shard"), check_vma=False)
```

```python
import functools

import jax
import jax.numpy as jnp
from jax import lax
from jax.experimental import pallas as pl
from jax.experimental.pallas import tpu as pltpu
from jax.sharding import PartitionSpec as P

MESH = pl.DeviceIdType.MESH
NT = (((1,), (1,)), ((), ()))
BLOCK = 128
SUB = 16
STEPS = 4
PER = BLOCK // SUB
PIECES = STEPS * PER
WINDOW = 6
DELAY = 8
LAG = 6

OWN = 0
KEYS = 2048
KEY_STEP = 3 * BLOCK
QRY = KEYS + STEPS * KEY_STEP
SIDE = QRY + STEPS * 2 * BLOCK
TOTAL = SIDE + STEPS * 2 * BLOCK

Y_KEY, Y_QRY, X_QRY, MISC = range(4)
X_KEY, S_KEY, S_QRY_A, S_QRY_X = range(4)


def scope(name):
    return jax.named_scope(name)


def kernel(shards, emb, labels, out, buf, klab, qlab, acc, lab, res, got_t, got_s, got_c, got_r,
           load_sem, piece_sem, step_sem, y_sent, sent_sem, misc_sent, hello):
    shard = lax.axis_index("shard")
    rep = lax.axis_index("rep")
    core = lax.rem(shard, 2)
    other = 1 - core
    chip2 = shard - core
    has_prev = chip2 > 0
    has_next = chip2 < shards - 2
    mid = has_prev & has_next
    sends_qry = chip2 > 2
    ahead = lax.rem(chip2 + 2, shards)
    behind = lax.rem(chip2 + shards - 2, shards)
    x_key = rep + 1 - 2 * lax.rem(rep, 2)
    x_qry = 3 - rep
    fwd, fwd_c = (ahead + core, rep), (ahead + other, rep)
    bwd, bwd_c = (behind + core, rep), (behind + other, rep)
    sib = (chip2 + other, rep)
    across = [(shard, lax.rem(rep + d, 4)) for d in (1, 2, 3)]
    first = (shard == 0) & (rep == 0)
    greeted = (shard == 0) & (rep > 0) | (shard == 1) & (rep == 0)

    def remote(src, dst, sent, got, device):
        return pltpu.make_async_remote_copy(
            src_ref=src, dst_ref=dst, send_sem=sent, recv_sem=got, device_id=device, device_id_type=MESH
        )

    def rows(start, count):
        return pl.ds(pl.multiple_of(start, SUB), count)

    def at(start, count=SUB):
        return buf.at[rows(start, count)]

    def key_step(q):
        return STEPS - 1 - q // PER

    def key_slot(q, slot):
        return KEYS + key_step(q) * KEY_STEP + slot * BLOCK + (q % PER) * SUB

    def qry_slot(base, q, slot):
        return base + (q // PER) * 2 * BLOCK + slot * BLOCK + (q % PER) * SUB

    def y_key(q):
        src = (4 * key_step(q) + rep) * BLOCK + (q % PER) * SUB
        return remote(at(src), at(key_slot(q, 1)), y_sent.at[0, q], piece_sem.at[Y_KEY, q], fwd)

    def y_qry(q):
        src = (4 * (q // PER) + rep) * BLOCK + (q % PER) * SUB
        return remote(at(src), at(qry_slot(QRY, q, 0)), y_sent.at[1, q], piece_sem.at[Y_QRY, q], bwd)

    def xq(q):
        dst = at(qry_slot(QRY, q, 1))
        return remote(at(qry_slot(QRY, q, 0)), dst, sent_sem.at[2], piece_sem.at[X_QRY, q], (shard, x_qry))

    def xk(q):
        dst = at(key_slot(q, 2))
        return remote(at(key_slot(q, 1)), dst, sent_sem.at[3], step_sem.at[X_KEY, q // PER], (shard, x_key))

    def s_key(q):
        return remote(at(key_slot(q, 1)), at(key_slot(q, 0)), sent_sem.at[4], step_sem.at[S_KEY, q // PER], sib)

    def s_qry(q, slot):
        src, dst = at(qry_slot(QRY, q, slot)), at(qry_slot(SIDE, q, slot))
        return remote(src, dst, sent_sem.at[5 + slot], step_sem.at[S_QRY_A + slot, q // PER], sib)

    def whole_step(kind, s):
        remote(at(0, BLOCK), at(0, BLOCK), sent_sem.at[0], step_sem.at[kind, s], sib).wait_recv()

    def all_sent(i):
        remote(at(0, PIECES * SUB), at(0, PIECES * SUB), sent_sem.at[i], step_sem.at[0, 0], sib).wait_send()

    def misc(src, dst, index, device):
        return remote(src, dst, misc_sent.at[index], piece_sem.at[MISC, index], device)

    def label_fwd():
        return [misc(labels, lab.at[i], i, d) for i, d in enumerate((fwd, fwd_c))]

    def label_bwd():
        return [misc(labels, lab.at[2 + i], 2 + i, d) for i, d in enumerate((bwd, bwd_c))]

    def label_sib():
        return misc(labels, lab.at[4], 4, sib)

    def side_block(j):
        return misc(at((4 * j + rep) * BLOCK, BLOCK), at(SIDE + j * BLOCK, BLOCK), 5 + j, sib)

    def cross_result():
        return misc(res.at[24:32], got_c, 9, sib)

    def spread(i):
        return misc(res.at[0:16], got_r.at[i], 10 + i, across[i])

    def qry_result(x):
        return remote(res.at[16:24], got_t.at[rep], misc_sent.at[13 + x], piece_sem.at[MISC, 13 + rep], (ahead + core, x))

    def side_result(x):
        return remote(res.at[24:32], got_s.at[rep], misc_sent.at[17 + x], piece_sem.at[MISC, 17 + rep], (ahead, x))

    def from_prev(kind, x):
        i, dst = ((13, got_t), (17, got_s))[kind]
        return remote(res.at[16:24], dst.at[x], misc_sent.at[i], piece_sem.at[MISC, i + x], fwd)

    def load(b, i):
        r = rows(b * BLOCK, BLOCK)
        return pltpu.make_async_copy(emb.at[r], buf.at[r], load_sem.at[i])

    mine = [4 * j + rep for j in (3, 0, 2, 1)]
    rest = [4 * j + lax.rem(rep + o, 4) for j in range(4) for o in (1, 2, 3)]
    order = mine + rest
    for i, b in enumerate(order):
        load(b, i).start()

    barrier = pltpu.get_barrier_semaphore()

    def greet(device):
        pl.semaphore_signal(barrier, inc=1, device_id=device, device_id_type=MESH)

    @pl.when(has_prev)
    def _():
        for x in range(4):
            for h in range(2):
                greet((behind + h, x))

    @pl.when(mid)
    def _():
        greet(fwd)
        greet(fwd_c)

    @pl.when(jnp.logical_not(first))
    def _():
        for device in [sib] + across:
            greet(device)

    def normalize(b):
        r = rows(b * BLOCK, BLOCK)
        total = jnp.zeros((BLOCK, 128), jnp.float32)
        for c in range(8):
            v = buf[r, c * 128:(c + 1) * 128].astype(jnp.float32)
            total = total + v * v
        mean = jnp.sum(total, axis=1, keepdims=True) * (1.0 / 1024.0)
        scale = jnp.broadcast_to(lax.rsqrt(mean + 1e-06), (BLOCK, 128))
        for c in range(8):
            v = buf[r, c * 128:(c + 1) * 128].astype(jnp.float32)
            buf[r, c * 128:(c + 1) * 128] = (v * scale * (1.0 / 32.0)).astype(jnp.bfloat16)

    def prepare(lo, hi):
        for i in range(lo, hi):
            load(order[i], i).wait()
            normalize(order[i])

    with scope("norm_first"):
        prepare(0, 2)
    with scope("barrier"):
        one = lambda flag: jnp.where(flag, 1, 0)
        pl.semaphore_wait(barrier, 8 * one(has_next) + 2 * one(sends_qry) + 4 - one(greeted))

        @pl.when(first)
        def _():
            for device in [sib] + across:
                pl.semaphore_signal(hello, inc=1, device_id=device, device_id_type=MESH)

    @pl.when(has_next)
    def _():
        for c in label_fwd():
            c.start()

    @pl.when(sends_qry)
    def _():
        for c in label_bwd():
            c.start()

    late_sib = first | (shard == 1) & (rep == 0)

    @pl.when(jnp.logical_not(late_sib))
    def _():
        label_sib().start()

    def send_y(q):
        @pl.when(mid if q >= WINDOW else has_next)
        def _():
            if q >= WINDOW:
                y_key(q - WINDOW).wait_send()
            y_key(q).start()

        @pl.when(sends_qry)
        def _():
            if q >= WINDOW:
                y_qry(q - WINDOW).wait_send()
            y_qry(q).start()

    for q in range(WINDOW):
        send_y(q)
    with scope("norm_mine"):
        prepare(2, 4)

    @pl.when((core == 1) & jnp.logical_not(late_sib))
    def _():
        for j in range(4):
            side_block(j).start()

    @pl.when(chip2 == 0)
    def _():
        for q in range(WINDOW, PIECES):
            y_key(q).start()

    with scope("norm_rest"):
        prepare(4, 16)

    def column(row, start):
        wide = jnp.broadcast_to(row, (BLOCK, BLOCK))
        klab[pl.ds(start, BLOCK), :] = wide.T

    def lab_row(i, r):
        return lab[i, pl.ds(r, 1), :]

    def own_labels():
        acc[...] = jnp.full_like(acc, -1.0)
        res[...] = jnp.full_like(res, -1.0)
        qlab[0:16, :] = labels[...]
        for b in range(16):
            column(labels[b:b + 1, :], b * BLOCK)

    def far_labels():
        @pl.when(has_prev)
        def _():
            for c in label_fwd():
                c.wait_recv()
            for j in range(4):
                a = 4 * j + rep
                column(lab_row(1, a), KEYS + j * KEY_STEP)
                column(lab_row(0, a), KEYS + j * KEY_STEP + BLOCK)
                column(lab_row(0, 4 * j + x_key), KEYS + j * KEY_STEP + 2 * BLOCK)

        @pl.when(mid)
        def _():
            for c in label_bwd():
                c.wait_recv()
            for j in range(4):
                s = QRY // BLOCK + 2 * j
                qlab[s:s + 1, :] = lab_row(2, 4 * j + rep)
                qlab[s + 1:s + 2, :] = lab_row(2, 4 * j + x_qry)

            @pl.when(core == 1)
            def _():
                for j in range(4):
                    s = SIDE // BLOCK + 2 * j
                    qlab[s:s + 1, :] = lab_row(3, 4 * j + rep)
                    qlab[s + 1:s + 2, :] = lab_row(3, 4 * j + x_qry)

    def sib_ready():
        @pl.when(late_sib)
        def _():
            @pl.when(core == 1)
            def _():
                pl.semaphore_wait(hello, 1)
                for j in range(4):
                    side_block(j).start()
            label_sib().start()

        label_sib().wait_recv()

        @pl.when(core == 0)
        def _():
            for j in range(4):
                qlab[SIDE // BLOCK + j:SIDE // BLOCK + j + 1, :] = lab_row(4, 4 * j + rep)
                side_block(j).wait_recv()

    def tile(key, qry, causal=False):
        key = pl.multiple_of(key, BLOCK)
        scores = lax.dot_general(
            buf[pl.ds(key, 256), :], buf[rows(qry, 256), :], NT, preferred_element_type=jnp.float32
        )
        lanes = klab[pl.ds(key, 256), :]
        for g in range(2):
            b = qry // BLOCK + g
            keep = lanes == qlab[pl.ds(b, 1), :]
            if causal:
                key_pos = key + lax.broadcasted_iota(jnp.int32, (256, BLOCK), 0)
                qry_pos = qry + g * BLOCK + lax.broadcasted_iota(jnp.int32, (256, BLOCK), 1)
                keep = keep & (key_pos < qry_pos)
            best = jnp.where(keep, scores[:, g * BLOCK:(g + 1) * BLOCK], jnp.float32(-1.0))
            best = jnp.max(best.reshape(32, 8, BLOCK), axis=0)
            a = pl.ds(pl.multiple_of(b * 8, 8), 8)
            acc[a, :] = jnp.maximum(acc[a, :], best)

    def key_tile(j):
        return KEYS + j * KEY_STEP

    def own_triangle(lo, hi):
        for i in range(lo, hi):
            low = i < 8 - rep
            key = jnp.where(low, rep, 7 - rep)
            qry = jnp.where(low, rep + i, i - 1)
            tile(key * 256, qry * 256, causal=True)

    def cross(lo, hi):
        @pl.when(core == 0)
        def _():
            for k in range(lo, hi):
                for t in range(2):
                    tile(k * 256, SIDE + t * 256)

    def best_rows(dst, block, count):
        for i in range(count):
            b = (block + i) * 8
            res[dst + i:dst + i + 1, :] = jnp.max(acc[b:b + 8, :], axis=0, keepdims=True)

    def cross_done():
        @pl.when(core == 0)
        def _():
            best_rows(24, SIDE // BLOCK, 4)
            cross_result().start()

    def near(s, lo, hi):
        @pl.when(has_prev)
        def _():
            if lo == 0:
                whole_step(S_KEY, s)
            for t in range(lo, hi):
                tile(key_tile(STEPS - 1 - s), OWN + t * 256)

    def far(s):
        j = STEPS - 1 - s

        @pl.when(mid)
        def _():
            whole_step(X_KEY, s)

            @pl.when(core == 1)
            def _():
                for q in range(s * PER, (s + 1) * PER):
                    xq(q).wait_recv()

            key = key_tile(j) + BLOCK
            for t in range(0, min(s, j) + 1):
                tile(key, QRY + t * 256)
            for k in range(max(s, j + 1), STEPS):
                tile(key_tile(k) + BLOCK, QRY + s * 256)

    def far_side(s):
        j = STEPS - 1 - s

        @pl.when(mid & (core == 1))
        def _():
            whole_step(S_QRY_A, s)
            whole_step(S_QRY_X, s)
            key = key_tile(j) + BLOCK
            for t in range(0, s + 1):
                tile(key, SIDE + t * 256)
            for k in range(j + 1, STEPS):
                tile(key_tile(k) + BLOCK, SIDE + s * 256)

    def relay(q):
        @pl.when(mid & (core == 0))
        def _():
            xq(q).wait_recv()
            s_qry(q, 1).start()

    def service(q):
        @pl.when(has_prev)
        def _():
            y_key(q).wait_recv()
            s_key(q).start()

        @pl.when(mid)
        def _():
            xk(q).start()
            y_qry(q).wait_recv()
            xq(q).start()

            @pl.when(core == 0)
            def _():
                s_qry(q, 0).start()

        if q >= LAG:
            relay(q - LAG)

    work = {q: [] for q in range(PIECES)}

    def plan(q, f, *a):
        work[q].append((f, a))

    plan(0, own_labels)
    plan(1, far_labels)
    for i in range(3):
        plan(2 + i, own_triangle, 3 * i, 3 * i + 3)
    plan(5, sib_ready)
    for i in range(4):
        plan(5 + i, cross, 2 * i, 2 * i + 2)
    plan(9, cross_done)
    for i in range(4):
        plan(10 + i, near, 0, 2 * i, 2 * i + 2)
        plan(17 + i, near, 1, 2 * i, 2 * i + 2)
    plan(25, near, 2, 0, 4)
    plan(26, near, 2, 4, 8)
    plan(15, far, 0)
    plan(21, far_side, 0)
    plan(23, far, 1)
    plan(27, far_side, 1)
    plan(29, far, 2)

    for q in range(WINDOW, DELAY):
        send_y(q)
    for q in range(PIECES):
        with scope("service%d" % q):
            if q + DELAY < PIECES:
                send_y(q + DELAY)
            service(q)
        with scope("work%d" % q):
            for f, a in work[q]:
                f(*a)

    with scope("tail_near"):
        for q in range(PIECES - LAG, PIECES - 2):
            relay(q)
        far_side(2)
        relay(PIECES - 2)
        near(3, 0, 4)
        relay(PIECES - 1)
        near(3, 4, 8)

    def merge(value, b):
        r = pl.ds(b, 1)
        res[r, :] = jnp.maximum(res[r, :], value)

    with scope("own_result"):
        best_rows(0, 0, 16)

        @pl.when(core == 1)
        def _():
            cross_result().wait_recv()
            for j in range(4):
                merge(got_c[j:j + 1, :], 4 * j + rep)

        @pl.when((core == 0) & greeted)
        def _():
            pl.semaphore_wait(hello, 1)

        for i in range(3):
            spread(i).start()

    with scope("tail_far"):
        far(3)

        @pl.when(mid)
        def _():
            best_rows(16, QRY // BLOCK, 8)
            for x in range(4):
                qry_result(x).start()

    with scope("tail_side"):
        far_side(3)

        @pl.when(mid & (core == 1))
        def _():
            best_rows(24, SIDE // BLOCK, 8)
            for x in range(4):
                side_result(x).start()

    with scope("spread_wait"):
        for i in range(3):
            spread(i).wait_recv()
        out[...] = jnp.maximum(jnp.maximum(res[0:16, :], got_r[0]), jnp.maximum(got_r[1], got_r[2]))

    def take(got):
        for r in range(4):
            for j in range(4):
                b = 4 * j + r
                best = jnp.maximum(got[r, 2 * j:2 * j + 1, :], got[3 - r, 2 * j + 1:2 * j + 2, :])
                out[b:b + 1, :] = jnp.maximum(out[b:b + 1, :], best)

    with scope("result_wait"):
        @pl.when(sends_qry)
        def _():
            for x in range(4):
                from_prev(0, x).wait_recv()
            take(got_t)

            @pl.when(core == 0)
            def _():
                for x in range(4):
                    from_prev(1, x).wait_recv()
                take(got_s)

    with scope("sent"):
        for i in range(3):
            spread(i).wait_send()
        label_sib().wait_send()

        @pl.when(has_next)
        def _():
            @pl.when(chip2 == 0)
            def _():
                for q in range(PIECES - WINDOW):
                    y_key(q).wait_send()
            for q in range(PIECES - WINDOW, PIECES):
                y_key(q).wait_send()
            for c in label_fwd():
                c.wait_send()

        @pl.when(sends_qry)
        def _():
            for q in range(PIECES - WINDOW, PIECES):
                y_qry(q).wait_send()
            for c in label_bwd():
                c.wait_send()

        @pl.when(has_prev)
        def _():
            all_sent(4)

        @pl.when(mid)
        def _():
            all_sent(2)
            all_sent(3)
            for x in range(4):
                qry_result(x).wait_send()

            @pl.when(core == 0)
            def _():
                all_sent(5)
                all_sent(6)

            @pl.when(core == 1)
            def _():
                for x in range(4):
                    side_result(x).wait_send()

        @pl.when(core == 0)
        def _():
            cross_result().wait_send()

        @pl.when(core == 1)
        def _():
            for j in range(4):
                side_block(j).wait_send()


def solution(mesh):
    shards = mesh.shape["shard"]

    def local(embeddings, labels):
        best = pl.pallas_call(
            functools.partial(kernel, shards),
            out_shape=jax.ShapeDtypeStruct((16, 128), jnp.float32),
            in_specs=[pl.BlockSpec(memory_space=pl.ANY), pl.BlockSpec(memory_space=pltpu.VMEM)],
            out_specs=pl.BlockSpec(memory_space=pltpu.VMEM),
            scratch_shapes=[
                pltpu.VMEM((TOTAL, 1024), jnp.bfloat16),
                pltpu.VMEM((QRY, BLOCK), jnp.int32),
                pltpu.VMEM((TOTAL // BLOCK, BLOCK), jnp.int32),
                pltpu.VMEM((TOTAL // BLOCK * 8, BLOCK), jnp.float32),
                pltpu.VMEM((5, 16, BLOCK), jnp.int32),
                pltpu.VMEM((32, BLOCK), jnp.float32),
                pltpu.VMEM((4, 8, BLOCK), jnp.float32),
                pltpu.VMEM((4, 8, BLOCK), jnp.float32),
                pltpu.VMEM((8, BLOCK), jnp.float32),
                pltpu.VMEM((3, 16, BLOCK), jnp.float32),
                pltpu.SemaphoreType.DMA((16,)),
                pltpu.SemaphoreType.DMA((4, 32)),
                pltpu.SemaphoreType.DMA((4, STEPS)),
                pltpu.SemaphoreType.DMA((2, 32)),
                pltpu.SemaphoreType.DMA((7,)),
                pltpu.SemaphoreType.DMA((21,)),
                pltpu.SemaphoreType.REGULAR,
            ],
            compiler_params=pltpu.CompilerParams(
                collective_id=0, has_side_effects=True, vmem_limit_bytes=56 * 2**20
            ),
        )(embeddings, labels.reshape(16, 128))
        return best.reshape(2048)

    placed = (P("shard", None), P("shard"))
    return jax.shard_map(local, mesh=mesh, in_specs=placed, out_specs=P("shard"), check_vma=False)
```

```python
import functools

import jax
import jax.numpy as jnp
from jax import lax
from jax.experimental import pallas as pl
from jax.experimental.pallas import tpu as pltpu
from jax.sharding import PartitionSpec as P

MESH = pl.DeviceIdType.MESH
NT = (((1,), (1,)), ((), ()))
BLOCK = 128
SUB = 16
STEPS = 4
PER = BLOCK // SUB
PIECES = STEPS * PER
WINDOW = 8
DELAY = 8
LAG = 6
DIRECT = 2

OWN = 0
KEYS = 2048
KEY_STEP = 3 * BLOCK
QRY = KEYS + STEPS * KEY_STEP
SIDE = QRY + STEPS * 2 * BLOCK
TOTAL = SIDE + STEPS * 2 * BLOCK

Y_KEY, Y_QRY, X_QRY, MISC = range(4)
X_KEY, S_KEY, S_QRY_A, S_QRY_X = range(4)


def scope(name):
    return jax.named_scope(name)


def kernel(shards, emb, labels, out, buf, klab, qlab, acc, lab, res, got_t, got_s, got_c, got_r,
           load_sem, piece_sem, step_sem, y_sent, sent_sem, misc_sent, hello):
    shard = lax.axis_index("shard")
    rep = lax.axis_index("rep")
    core = lax.rem(shard, 2)
    other = 1 - core
    chip2 = shard - core
    has_prev = chip2 > 0
    has_next = chip2 < shards - 2
    mid = has_prev & has_next
    sends_qry = chip2 > 2
    ahead = lax.rem(chip2 + 2, shards)
    behind = lax.rem(chip2 + shards - 2, shards)
    x_key = rep + 1 - 2 * lax.rem(rep, 2)
    x_qry = 3 - rep
    fwd, fwd_c = (ahead + core, rep), (ahead + other, rep)
    bwd, bwd_c = (behind + core, rep), (behind + other, rep)
    sib = (chip2 + other, rep)
    across = [(shard, lax.rem(rep + d, 4)) for d in (1, 2, 3)]
    first = (shard == 0) & (rep == 0)
    greeted = (shard == 0) & (rep > 0) | (shard == 1) & (rep == 0)

    def remote(src, dst, sent, got, device):
        return pltpu.make_async_remote_copy(
            src_ref=src, dst_ref=dst, send_sem=sent, recv_sem=got, device_id=device, device_id_type=MESH
        )

    def rows(start, count):
        return pl.ds(pl.multiple_of(start, SUB), count)

    def at(start, count=SUB):
        return buf.at[rows(start, count)]

    def key_step(q):
        return STEPS - 1 - q // PER

    def key_slot(q, slot):
        return KEYS + key_step(q) * KEY_STEP + slot * BLOCK + (q % PER) * SUB

    def qry_slot(base, q, slot):
        return base + (q // PER) * 2 * BLOCK + slot * BLOCK + (q % PER) * SUB

    def y_key(q):
        src = (4 * key_step(q) + rep) * BLOCK + (q % PER) * SUB
        return remote(at(src), at(key_slot(q, 1)), y_sent.at[0, q], piece_sem.at[Y_KEY, q], fwd)

    def y_qry(q):
        src = (4 * (q // PER) + rep) * BLOCK + (q % PER) * SUB
        return remote(at(src), at(qry_slot(QRY, q, 0)), y_sent.at[1, q], piece_sem.at[Y_QRY, q], bwd)

    def xq(q):
        dst = at(qry_slot(QRY, q, 1))
        return remote(at(qry_slot(QRY, q, 0)), dst, sent_sem.at[2], piece_sem.at[X_QRY, q], (shard, x_qry))

    def xk(q):
        dst = at(key_slot(q, 2))
        return remote(at(key_slot(q, 1)), dst, sent_sem.at[3], step_sem.at[X_KEY, q // PER], (shard, x_key))

    def s_key(q):
        return remote(at(key_slot(q, 1)), at(key_slot(q, 0)), sent_sem.at[4], step_sem.at[S_KEY, q // PER], sib)

    def s_qry(q, slot):
        src, dst = at(qry_slot(QRY, q, slot)), at(qry_slot(SIDE, q, slot))
        return remote(src, dst, sent_sem.at[5 + slot], step_sem.at[S_QRY_A + slot, q // PER], sib)

    def xq_side(q):
        dst = at(qry_slot(SIDE, q, 1))
        return remote(at(qry_slot(QRY, q, 0)), dst, sent_sem.at[6], step_sem.at[S_QRY_X, q // PER], (chip2 + other, x_qry))

    def whole_step(kind, s):
        remote(at(0, BLOCK), at(0, BLOCK), sent_sem.at[0], step_sem.at[kind, s], sib).wait_recv()

    def all_sent(i):
        remote(at(0, PIECES * SUB), at(0, PIECES * SUB), sent_sem.at[i], step_sem.at[0, 0], sib).wait_send()

    def misc(src, dst, index, device):
        return remote(src, dst, misc_sent.at[index], piece_sem.at[MISC, index], device)

    def label_fwd():
        return [misc(labels, lab.at[i], i, d) for i, d in enumerate((fwd, fwd_c))]

    def label_bwd():
        return [misc(labels, lab.at[2 + i], 2 + i, d) for i, d in enumerate((bwd, bwd_c))]

    def label_sib():
        return misc(labels, lab.at[4], 4, sib)

    def side_block(j):
        return misc(at((4 * j + rep) * BLOCK, BLOCK), at(SIDE + j * BLOCK, BLOCK), 5 + j, sib)

    def cross_result():
        return misc(res.at[24:32], got_c, 9, sib)

    def spread(i):
        return misc(res.at[0:16], got_r.at[i], 10 + i, across[i])

    def qry_result(x):
        return remote(res.at[16:24], got_t.at[rep], misc_sent.at[13 + x], piece_sem.at[MISC, 13 + rep], (ahead + core, x))

    def side_result(x):
        return remote(res.at[24:32], got_s.at[rep], misc_sent.at[17 + x], piece_sem.at[MISC, 17 + rep], (ahead, x))

    def from_prev(kind, x):
        i, dst = ((13, got_t), (17, got_s))[kind]
        return remote(res.at[16:24], dst.at[x], misc_sent.at[i], piece_sem.at[MISC, i + x], fwd)

    def load(b, i):
        r = rows(b * BLOCK, BLOCK)
        return pltpu.make_async_copy(emb.at[r], buf.at[r], load_sem.at[i])

    mine = [4 * j + rep for j in (3, 0, 2, 1)]
    rest = [4 * j + lax.rem(rep + o, 4) for j in range(4) for o in (1, 2, 3)]
    order = mine + rest
    for i in range(4):
        load(order[i], i).start()

    barrier = pltpu.get_barrier_semaphore()

    def greet(device):
        pl.semaphore_signal(barrier, inc=1, device_id=device, device_id_type=MESH)

    @pl.when(has_prev)
    def _():
        for x in range(4):
            for h in range(2):
                greet((behind + h, x))

    @pl.when(mid)
    def _():
        greet(fwd)
        greet(fwd_c)

        @pl.when(core == 1)
        def _():
            greet((chip2, x_qry))

    @pl.when(jnp.logical_not(first))
    def _():
        for device in [sib] + across:
            greet(device)

    def normalize(b):
        r = rows(b * BLOCK, BLOCK)
        total = jnp.zeros((BLOCK, 128), jnp.float32)
        for c in range(8):
            v = buf[r, c * 128:(c + 1) * 128].astype(jnp.float32)
            total = total + v * v
        mean = jnp.sum(total, axis=1, keepdims=True) * (1.0 / 1024.0)
        scale = jnp.broadcast_to(lax.rsqrt(mean + 1e-06), (BLOCK, 128))
        for c in range(8):
            v = buf[r, c * 128:(c + 1) * 128].astype(jnp.float32)
            buf[r, c * 128:(c + 1) * 128] = (v * scale * (1.0 / 32.0)).astype(jnp.bfloat16)

    def prepare(lo, hi):
        for i in range(lo, hi):
            load(order[i], i).wait()
            normalize(order[i])

    with scope("norm_first"):
        prepare(0, 2)
    with scope("barrier"):
        one = lambda flag: jnp.where(flag, 1, 0)
        pl.semaphore_wait(barrier, 8 * one(has_next) + 2 * one(sends_qry) + 4 + one(mid & (core == 0)) - one(greeted))

        @pl.when(first)
        def _():
            for device in [sib] + across:
                pl.semaphore_signal(hello, inc=1, device_id=device, device_id_type=MESH)

    @pl.when(has_next)
    def _():
        for c in label_fwd():
            c.start()

    @pl.when(sends_qry)
    def _():
        for c in label_bwd():
            c.start()

    late_sib = first | (shard == 1) & (rep == 0)

    @pl.when(jnp.logical_not(late_sib))
    def _():
        label_sib().start()

    def send_y(q):
        @pl.when(mid if q >= WINDOW else has_next)
        def _():
            if q >= WINDOW:
                y_key(q - WINDOW).wait_send()
            y_key(q).start()

        @pl.when(sends_qry)
        def _():
            if q >= WINDOW:
                y_qry(q - WINDOW).wait_send()
            y_qry(q).start()

    for q in range(WINDOW):
        send_y(q)
    for i in range(4, 16):
        load(order[i], i).start()
    with scope("norm_mine"):
        prepare(2, 4)

    @pl.when((core == 1) & jnp.logical_not(late_sib))
    def _():
        for j in range(4):
            side_block(j).start()

    @pl.when(chip2 == 0)
    def _():
        for q in range(WINDOW, PIECES):
            y_key(q).start()

    with scope("norm_rest"):
        prepare(4, 16)

    def column(row, start):
        wide = jnp.broadcast_to(row, (BLOCK, BLOCK))
        klab[pl.ds(start, BLOCK), :] = wide.T

    def lab_row(i, r):
        return lab[i, pl.ds(r, 1), :]

    def own_labels():
        acc[...] = jnp.full_like(acc, -1.0)
        res[...] = jnp.full_like(res, -1.0)
        qlab[0:16, :] = labels[...]
        for b in range(16):
            column(labels[b:b + 1, :], b * BLOCK)

    def far_labels():
        @pl.when(has_prev)
        def _():
            for c in label_fwd():
                c.wait_recv()
            for j in range(4):
                a = 4 * j + rep
                column(lab_row(1, a), KEYS + j * KEY_STEP)
                column(lab_row(0, a), KEYS + j * KEY_STEP + BLOCK)
                column(lab_row(0, 4 * j + x_key), KEYS + j * KEY_STEP + 2 * BLOCK)

        @pl.when(mid)
        def _():
            for c in label_bwd():
                c.wait_recv()
            for j in range(4):
                s = QRY // BLOCK + 2 * j
                qlab[s:s + 1, :] = lab_row(2, 4 * j + rep)
                qlab[s + 1:s + 2, :] = lab_row(2, 4 * j + x_qry)

            @pl.when(core == 1)
            def _():
                for j in range(4):
                    s = SIDE // BLOCK + 2 * j
                    qlab[s:s + 1, :] = lab_row(3, 4 * j + rep)
                    qlab[s + 1:s + 2, :] = lab_row(3, 4 * j + x_qry)

    def sib_ready():
        @pl.when(late_sib)
        def _():
            @pl.when(core == 1)
            def _():
                pl.semaphore_wait(hello, 1)
                for j in range(4):
                    side_block(j).start()
            label_sib().start()

        label_sib().wait_recv()

        @pl.when(core == 0)
        def _():
            for j in range(4):
                qlab[SIDE // BLOCK + j:SIDE // BLOCK + j + 1, :] = lab_row(4, 4 * j + rep)
                side_block(j).wait_recv()

    def tile(key, qry, causal=False):
        key = pl.multiple_of(key, BLOCK)
        scores = lax.dot_general(
            buf[pl.ds(key, 256), :], buf[rows(qry, 256), :], NT, preferred_element_type=jnp.float32
        )
        lanes = klab[pl.ds(key, 256), :]
        for g in range(2):
            b = qry // BLOCK + g
            keep = lanes == qlab[pl.ds(b, 1), :]
            if causal:
                key_pos = key + lax.broadcasted_iota(jnp.int32, (256, BLOCK), 0)
                qry_pos = qry + g * BLOCK + lax.broadcasted_iota(jnp.int32, (256, BLOCK), 1)
                keep = keep & (key_pos < qry_pos)
            best = jnp.where(keep, scores[:, g * BLOCK:(g + 1) * BLOCK], jnp.float32(-1.0))
            best = jnp.max(best.reshape(32, 8, BLOCK), axis=0)
            a = pl.ds(pl.multiple_of(b * 8, 8), 8)
            acc[a, :] = jnp.maximum(acc[a, :], best)

    def key_tile(j):
        return KEYS + j * KEY_STEP

    def own_triangle(lo, hi):
        for i in range(lo, hi):
            low = i < 8 - rep
            key = jnp.where(low, rep, 7 - rep)
            qry = jnp.where(low, rep + i, i - 1)
            tile(key * 256, qry * 256, causal=True)

    def cross(lo, hi):
        @pl.when(core == 0)
        def _():
            for k in range(lo, hi):
                for t in range(2):
                    tile(k * 256, SIDE + t * 256)

    def best_rows(dst, block, count):
        for i in range(count):
            b = (block + i) * 8
            res[dst + i:dst + i + 1, :] = jnp.max(acc[b:b + 8, :], axis=0, keepdims=True)

    def cross_done():
        @pl.when(core == 0)
        def _():
            best_rows(24, SIDE // BLOCK, 4)
            cross_result().start()

    def near(s, lo, hi):
        @pl.when(has_prev)
        def _():
            if lo == 0:
                whole_step(S_KEY, s)
            for t in range(lo, hi):
                tile(key_tile(STEPS - 1 - s), OWN + t * 256)

    def far(s):
        j = STEPS - 1 - s

        @pl.when(mid)
        def _():
            whole_step(X_KEY, s)

            @pl.when(core == 1)
            def _():
                for q in range(s * PER, (s + 1) * PER):
                    xq(q).wait_recv()

            key = key_tile(j) + BLOCK
            for t in range(0, min(s, j) + 1):
                tile(key, QRY + t * 256)
            for k in range(max(s, j + 1), STEPS):
                tile(key_tile(k) + BLOCK, QRY + s * 256)

    def far_side(s):
        j = STEPS - 1 - s

        @pl.when(mid & (core == 1))
        def _():
            whole_step(S_QRY_A, s)
            whole_step(S_QRY_X, s)
            key = key_tile(j) + BLOCK
            for t in range(0, s + 1):
                tile(key, SIDE + t * 256)
            for k in range(j + 1, STEPS):
                tile(key_tile(k) + BLOCK, SIDE + s * 256)

    def relay(q):
        @pl.when(mid & (core == 0))
        def _():
            xq(q).wait_recv()
            if q < PIECES - DIRECT:
                s_qry(q, 1).start()

    def service(q):
        @pl.when(has_prev)
        def _():
            y_key(q).wait_recv()
            s_key(q).start()

        @pl.when(mid)
        def _():
            xk(q).start()
            y_qry(q).wait_recv()
            xq(q).start()

            @pl.when(core == 0)
            def _():
                if q >= PIECES - DIRECT:
                    xq_side(q).start()
                s_qry(q, 0).start()

        if q >= LAG:
            relay(q - LAG)

    work = {q: [] for q in range(PIECES)}

    def plan(q, f, *a):
        work[q].append((f, a))

    plan(0, own_labels)
    plan(1, far_labels)
    for i in range(3):
        plan(2 + 2 * i, own_triangle, 3 * i, 3 * i + 3)
    plan(7, sib_ready)
    plan(8, cross, 0, 2)
    plan(10, cross, 2, 4)
    plan(11, near, 0, 0, 4)
    plan(13, near, 0, 4, 8)
    plan(14, cross, 4, 6)
    plan(16, cross, 6, 8)
    plan(17, far, 0)
    plan(17, cross_done)
    plan(18, near, 1, 0, 4)
    plan(19, far_side, 0)
    plan(20, near, 1, 4, 8)
    plan(23, far, 1)
    plan(25, near, 2, 0, 4)
    plan(26, far_side, 1)
    plan(27, near, 2, 4, 8)
    plan(29, far, 2)

    for q in range(WINDOW, DELAY):
        send_y(q)
    for q in range(PIECES):
        with scope("service%d" % q):
            if q + DELAY < PIECES:
                send_y(q + DELAY)
            service(q)
        with scope("work%d" % q):
            for f, a in work[q]:
                f(*a)

    with scope("tail_near"):
        for q in range(PIECES - LAG, PIECES - 2):
            relay(q)
        far_side(2)
        relay(PIECES - 2)
        near(3, 0, 4)
        relay(PIECES - 1)
        near(3, 4, 8)

    def merge(value, b):
        r = pl.ds(b, 1)
        res[r, :] = jnp.maximum(res[r, :], value)

    with scope("own_result"):
        best_rows(0, 0, 16)

        @pl.when(core == 1)
        def _():
            cross_result().wait_recv()
            for j in range(4):
                merge(got_c[j:j + 1, :], 4 * j + rep)

        @pl.when((core == 0) & greeted)
        def _():
            pl.semaphore_wait(hello, 1)

        for i in range(3):
            spread(i).start()

    with scope("tail_far"):
        far(3)

        @pl.when(mid)
        def _():
            best_rows(16, QRY // BLOCK, 8)
            for x in range(4):
                qry_result(x).start()

    with scope("tail_side"):
        far_side(3)

        @pl.when(mid & (core == 1))
        def _():
            best_rows(24, SIDE // BLOCK, 8)
            for x in range(4):
                side_result(x).start()

    with scope("spread_wait"):
        for i in range(3):
            spread(i).wait_recv()
        out[...] = jnp.maximum(jnp.maximum(res[0:16, :], got_r[0]), jnp.maximum(got_r[1], got_r[2]))

    def take(got):
        for r in range(4):
            for j in range(4):
                b = 4 * j + r
                best = jnp.maximum(got[r, 2 * j:2 * j + 1, :], got[3 - r, 2 * j + 1:2 * j + 2, :])
                out[b:b + 1, :] = jnp.maximum(out[b:b + 1, :], best)

    with scope("result_wait"):
        @pl.when(sends_qry)
        def _():
            for x in range(4):
                from_prev(0, x).wait_recv()
            take(got_t)

            @pl.when(core == 0)
            def _():
                for x in range(4):
                    from_prev(1, x).wait_recv()
                take(got_s)

    with scope("sent"):
        for i in range(3):
            spread(i).wait_send()
        label_sib().wait_send()

        @pl.when(has_next)
        def _():
            @pl.when(chip2 == 0)
            def _():
                for q in range(PIECES - WINDOW):
                    y_key(q).wait_send()
            for q in range(PIECES - WINDOW, PIECES):
                y_key(q).wait_send()
            for c in label_fwd():
                c.wait_send()

        @pl.when(sends_qry)
        def _():
            for q in range(PIECES - WINDOW, PIECES):
                y_qry(q).wait_send()
            for c in label_bwd():
                c.wait_send()

        @pl.when(has_prev)
        def _():
            all_sent(4)

        @pl.when(mid)
        def _():
            all_sent(2)
            all_sent(3)
            for x in range(4):
                qry_result(x).wait_send()

            @pl.when(core == 0)
            def _():
                all_sent(5)
                all_sent(6)

            @pl.when(core == 1)
            def _():
                for x in range(4):
                    side_result(x).wait_send()

        @pl.when(core == 0)
        def _():
            cross_result().wait_send()

        @pl.when(core == 1)
        def _():
            for j in range(4):
                side_block(j).wait_send()


def solution(mesh):
    shards = mesh.shape["shard"]

    def local(embeddings, labels):
        best = pl.pallas_call(
            functools.partial(kernel, shards),
            out_shape=jax.ShapeDtypeStruct((16, 128), jnp.float32),
            in_specs=[pl.BlockSpec(memory_space=pl.ANY), pl.BlockSpec(memory_space=pltpu.VMEM)],
            out_specs=pl.BlockSpec(memory_space=pltpu.VMEM),
            scratch_shapes=[
                pltpu.VMEM((TOTAL, 1024), jnp.bfloat16),
                pltpu.VMEM((QRY, BLOCK), jnp.int32),
                pltpu.VMEM((TOTAL // BLOCK, BLOCK), jnp.int32),
                pltpu.VMEM((TOTAL // BLOCK * 8, BLOCK), jnp.float32),
                pltpu.VMEM((5, 16, BLOCK), jnp.int32),
                pltpu.VMEM((32, BLOCK), jnp.float32),
                pltpu.VMEM((4, 8, BLOCK), jnp.float32),
                pltpu.VMEM((4, 8, BLOCK), jnp.float32),
                pltpu.VMEM((8, BLOCK), jnp.float32),
                pltpu.VMEM((3, 16, BLOCK), jnp.float32),
                pltpu.SemaphoreType.DMA((16,)),
                pltpu.SemaphoreType.DMA((4, 32)),
                pltpu.SemaphoreType.DMA((4, STEPS)),
                pltpu.SemaphoreType.DMA((2, 32)),
                pltpu.SemaphoreType.DMA((7,)),
                pltpu.SemaphoreType.DMA((21,)),
                pltpu.SemaphoreType.REGULAR,
            ],
            compiler_params=pltpu.CompilerParams(
                collective_id=0, has_side_effects=True, vmem_limit_bytes=56 * 2**20
            ),
        )(embeddings, labels.reshape(16, 128))
        return best.reshape(2048)

    placed = (P("shard", None), P("shard"))
    return jax.shard_map(local, mesh=mesh, in_specs=placed, out_specs=P("shard"), check_vma=False)
```
